32 devices in a mesh: groups: 2 (over y), rows: 4 (over z), cols: 2 (over x), sub: 2 (over core).
Axes of the slice: x: 2, y: 2, z: 4, core: 2. Of those that a mesh axis runs over, the one named last changes fastest.
Arguments:
- elevation: float32 [256, 16384], P(('groups', 'rows', 'sub'), 'cols'), parts along dimension 0, may hold values from -6 to 6
- fill_depth: float32 [256, 16384], P(('groups', 'rows', 'sub'), 'cols'), parts along dimension 0, may hold values from 0.5 to 4
- edge_rows: int32 [4, 16384], P('groups', 'cols'), parts along dimension 0, may hold values 0 or 1
- edge_sides: int32 [4, 128], P('groups', ('rows', 'sub')), parts along dimension 0, may hold values 0 or 1
- adjacency: int32 [16, 6], P('groups'), parts along dimension 0, may hold values from 0 to 7
Outputs:
- filled: float32 [256, 16384], P(('groups', 'rows', 'sub'), 'cols'), parts along dimension 0
The draws below stay inside these ranges and needn't reach their ends.
There are 2 independent parts, one for each index of `groups`. The reference program is written for one: setup_inputs(seed, part) draws one part's arguments, and reference() takes and returns one part's arrays. A program takes and returns all parts, laid end to end along the dimension named above; each array names one. Nothing has to cross between parts.
Inputs may be any that keep to these rules, and one draw needn't show every extreme that they name: `adjacency`: tile numbers count tiles row by row.
All inputs are finite; a program needn't handle non-finite values. No bound on the sum of `edge_rows` or of `edge_sides` on one device may be relied on, other than what follows from the above.
Results may differ from the reference program's by a relative error of at most 0.00002.
Values sent between devices are 32-bit elements; how exact they have to be, the bound alone decides.
A program may use at most 64 MiB of HBM per device.

```python
import math
import jax
import jax.numpy as jnp

PASSES = 8
FINAL = 4
ROUNDS = 4
DEG = 6
NR = 128
NC = 16384
TILES = 8
N_ROWS = 4
N_COLS = 2


def with_ends(drawn, own_key, smallest, largest):
    shape = drawn.shape
    place = [jax.random.randint(jax.random.fold_in(own_key, axis), (), 0, shape[axis]) for axis in range(len(shape))]
    drawn = drawn.at[tuple(place)].set(smallest)
    longest = shape.index(max(shape))
    place[longest] = (place[longest] + 1) % shape[longest]
    return drawn.at[tuple(place)].set(largest)


def steps_of(stream_key, shape, pieces, least, largest):
    def one(dim, blocks):
        draws = jax.random.uniform(jax.random.fold_in(jax.random.fold_in(stream_key, 6), dim), (blocks,), jnp.float32, least / len(pieces), largest / len(pieces))
        return jnp.repeat(jnp.exp(draws), shape[dim] // blocks).reshape((-1,) + (1,) * (len(shape) - dim - 1))

    factor_of = one(*pieces[0])
    for cut in pieces[1:]:
        factor_of = factor_of * one(*cut)
    return factor_of


def noise(key, shape, scale, limit, split=(), dtype=jnp.bfloat16):
    array = jax.random.normal(key, shape, jnp.float32) * scale
    if len(split) > 0:
        array = steps_of(key, shape, split, -0.22, 0.18) * array
    return jnp.clip(array, min=-limit, max=limit).astype(dtype)


def setup_inputs(seed: int = 0, part: int = 0) -> dict:
    seeds = jax.random.split(jax.random.key(seed), 6)
    part_keys = jax.random.split(jax.random.fold_in(seeds[5], part), 6)
    elevation = noise(part_keys[0], (NR, NC), 1.0, 6.0, ((0, 8), (1, 2)), jnp.float32)
    fill_depth = jnp.clip(jnp.exp(math.log(4.0) - 2.0794415 * jax.random.uniform(part_keys[1], (NR, NC), jnp.float32) ** steps_of(part_keys[1], (NR, NC), ((0, 8), (1, 2)), -0.2, 0.2)), 0.5, 4.0)
    edge_rows = with_ends((jax.random.randint(part_keys[2], (2, NC), 0, 8) < 1).astype(jnp.int32), jax.random.fold_in(part_keys[2], 1), 0, 1)
    edge_sides = with_ends((jax.random.randint(part_keys[3], (2, NR), 0, 8) < 1).astype(jnp.int32), jax.random.fold_in(part_keys[3], 1), 0, 1)
    adjacency = with_ends(jax.random.randint(part_keys[4], (TILES, DEG), 0, TILES), jax.random.fold_in(part_keys[4], 1), 0, TILES - 1).astype(jnp.int32)
    return dict(elevation=elevation, fill_depth=fill_depth, edge_rows=edge_rows, edge_sides=edge_sides, adjacency=adjacency)


unreached = 1.0e9
rise_step = 0.01
hop_rise = 0.05
spill_lift = 3.0


def neighbour_min(padded):
    height = padded.shape[0] - 2
    width = padded.shape[1] - 2
    lowest = None
    for shift_row in range(3):
        for shift_col in range(3):
            if shift_row == 1 and shift_col == 1:
                continue
            piece = padded[shift_row:shift_row + height, shift_col:shift_col + width]
            lowest = piece if lowest is None else jnp.minimum(lowest, piece)
    return lowest


def relax(surface, ground):
    padded = jnp.pad(surface, 1, constant_values=unreached)
    lowest = neighbour_min(padded)
    return jnp.maximum(ground, jnp.minimum(surface, lowest + rise_step))


def reference(elevation, fill_depth, edge_rows, edge_sides, adjacency):
    total_rows, total_cols = elevation.shape
    row_ids = jnp.arange(total_rows)[:, None]
    col_ids = jnp.arange(total_cols)[None, :]
    outlet = ((row_ids == 0) & (edge_rows[0][None, :] == 1)) | ((row_ids == total_rows - 1) & (edge_rows[1][None, :] == 1))
    outlet = outlet | ((col_ids == 0) & (edge_sides[0][:, None] == 1)) | ((col_ids == total_cols - 1) & (edge_sides[1][:, None] == 1))
    surface = jnp.where(outlet, elevation, elevation + fill_depth)
    for step in range(PASSES):
        surface = relax(surface, elevation)
    tile_rows = total_rows // N_ROWS
    tile_cols = total_cols // N_COLS
    blocks = surface.reshape(N_ROWS, tile_rows, N_COLS, tile_cols)
    floors = jnp.minimum(jnp.min(blocks[:, 0, :, :], axis=-1), jnp.min(blocks[:, -1, :, :], axis=-1))
    floors = jnp.minimum(floors, jnp.min(blocks[:, :, :, 0], axis=1))
    floors = jnp.minimum(floors, jnp.min(blocks[:, :, :, -1], axis=1))
    level = floors.reshape(N_ROWS * N_COLS)
    for step in range(ROUNDS):
        level = jnp.minimum(level, jnp.min(level[adjacency], axis=1) + hop_rise)
    ceiling = (level + spill_lift).reshape(N_ROWS, 1, N_COLS, 1)
    blocks = jnp.maximum(elevation.reshape(N_ROWS, tile_rows, N_COLS, tile_cols), jnp.minimum(blocks, ceiling))
    surface = blocks.reshape(total_rows, total_cols)
    for step in range(FINAL):
        surface = relax(surface, elevation)
    return surface
```

```python
import functools

import jax
import jax.numpy as jnp
from jax import lax
from jax.experimental import pallas as pl
from jax.experimental.pallas import tpu as pltpu
from jax.sharding import PartitionSpec as P

PASSES = 8
ROUNDS = 4

unreached = 1000000000.0
rise_step = 0.01
hop_rise = 0.05
spill_lift = 3.0

DEPTH = 4
SUBL = 8
TILE = 128
HALF = TILE // 2
MESH = pl.DeviceIdType.MESH


def kernel(
    sizes, elev_hbm, fill_hbm, edge_hbm, side_hbm, adj_hbm, out_hbm,
    ground, fill, first, second, third, ping, pong, done,
    edge, side, adj, ring_own, ring_low, ring_high,
    mine, gathered, hops, levels,
    load_sem, send_sem, recv_sem, level_send, level_recv, out_sem,
):
    n_groups, n_rows, n_cols, n_sub = sizes
    height, width = elev_hbm.shape
    chunk = width // SUBL
    lanes = chunk + TILE
    low, high = DEPTH, DEPTH + height
    total = height + 2 * DEPTH
    n_tiles = adj.shape[0]
    padded = mine.shape[1]
    members = n_rows * n_cols * n_sub

    group = lax.axis_index("groups")
    tile_row = lax.axis_index("rows")
    col = lax.axis_index("cols")
    sub = lax.axis_index("sub")
    band = tile_row * n_sub + sub
    bands = n_rows * n_sub
    me = (tile_row * n_cols + col) * n_sub + sub

    has = {-1: band > 0, 1: band < bands - 1, 0: True}
    has_col = {-1: col > 0, 1: col < n_cols - 1, 0: True}

    def both(dr, dc):
        if dr == 0:
            return has_col[dc]
        if dc == 0:
            return has[dr]
        return jnp.logical_and(has[dr], has_col[dc])

    def device(dr, dc):
        to_band = band + dr
        return (group, to_band // n_sub, col + dc, to_band % n_sub)

    loads = []
    for number, (src, dst, at) in enumerate(
        ((elev_hbm, ground, low), (fill_hbm, fill, 0), (edge_hbm, edge, 0))
    ):
        count = src.shape[0]
        for s in range(SUBL):
            pltpu.make_async_copy(
                src.at[:, pl.ds(s * chunk, chunk)],
                dst.at[pl.ds(at, count), s, pl.ds(0, chunk)],
                load_sem.at[number],
            ).start()
        whole = dst.at[pl.ds(at, count), :, pl.ds(0, chunk)]
        loads.append(pltpu.make_async_copy(whole, whole, load_sem.at[number]))
    side_load = pltpu.make_async_copy(side_hbm, side, load_sem.at[3])
    side_load.start()
    adj_load = pltpu.make_async_copy(adj_hbm, adj, load_sem.at[4])
    adj_load.start()

    barrier = pltpu.get_barrier_semaphore()

    def member(number):
        return (group, number // (n_sub * n_cols), (number // n_sub) % n_cols, number % n_sub)

    def greet(step, carry):
        pl.semaphore_signal(
            barrier, inc=1, device_id=member((me + step) % members), device_id_type=MESH
        )
        return carry

    lax.fori_loop(1, members, greet, 0)

    def outside_rows(at):
        for ref in (ground, first, second, third):
            ref[pl.ds(at, DEPTH)] = jnp.full((DEPTH, SUBL, lanes), unreached, jnp.float32)

    pl.when(jnp.logical_not(has[-1]))(lambda: outside_rows(0))
    pl.when(jnp.logical_not(has[1]))(lambda: outside_rows(high))

    spans = {-1: (0, DEPTH), 0: (low, height), 1: (high, DEPTH)}
    for dc, ref in ((-1, ring_low), (1, ring_high)):
        for dr in (-1, 0, 1):

            def outside_ring(ref=ref, dr=dr):
                at, count = spans[dr]
                ref[:, pl.ds(at, count)] = jnp.full((2, count, 1, TILE), unreached, jnp.float32)

            pl.when(jnp.logical_not(both(dr, dc)))(outside_ring)

    adj_load.wait()
    lane_tile = lax.broadcasted_iota(jnp.int32, (n_tiles, padded), 1)
    linked = jnp.zeros((n_tiles, padded), jnp.float32)
    links = adj[...]
    for k in range(links.shape[1]):
        linked = jnp.where(links[:, k : k + 1] == lane_tile, 1.0, linked)
    own = lax.broadcasted_iota(jnp.int32, (n_tiles, padded), 0) == lane_tile
    linked = jnp.where(own, 1.0, linked)
    one_hop = linked
    if n_tiles < padded:
        one_hop = jnp.concatenate(
            [one_hop, jnp.zeros((padded - n_tiles, padded), jnp.float32)], axis=0
        )
    count = jnp.where(own, 0.0, 1.0)
    reach = linked
    for step in range(ROUNDS):
        count = count + (1.0 - reach)
        if step < ROUNDS - 1:
            reach = jnp.dot(reach, one_hop, preferred_element_type=jnp.float32)
            reach = jnp.where(reach > 0.5, 1.0, 0.0)
    hops[...] = count

    sub_id = lax.broadcasted_iota(jnp.int32, (SUBL, TILE), 0)
    lane_id = lax.broadcasted_iota(jnp.int32, (SUBL, TILE), 1)
    first_cell = jnp.logical_and(sub_id == 0, lane_id == 0)
    last_cell = jnp.logical_and(sub_id == SUBL - 1, lane_id == TILE - 1)
    is_first_col = (col == 0).astype(jnp.int32)
    is_last_col = (col == n_cols - 1).astype(jnp.int32)
    top_mark = jnp.where(band == 0, 1, 2)
    bottom_mark = jnp.where(band == bands - 1, 1, 2)
    right_half = lane_id < HALF

    def ring_of(ref, r):
        left_tile = ref[r, :, 0:TILE]
        right_tile = ref[r, :, chunk - TILE : chunk]
        return jnp.where(
            right_half, pltpu.roll(left_tile, SUBL - 1, 0), pltpu.roll(right_tile, 1, 0)
        )

    side_load.wait()
    for load in loads:
        load.wait()

    def start_row(i):
        height_row = ground[low + i, :, 0:chunk]
        water = height_row + fill[i]
        if i == 0:
            water = jnp.where(edge[0] == top_mark, height_row, water)
        if i == height - 1:
            water = jnp.where(edge[1] == bottom_mark, height_row, water)
        first[low + i, :, 0:chunk] = water
        mark = jnp.where(first_cell, side[0, i] * is_first_col, 0) == 1
        first[low + i, :, 0:TILE] = jnp.where(
            mark, ground[low + i, :, 0:TILE], first[low + i, :, 0:TILE]
        )
        at = chunk - TILE
        mark = jnp.where(last_cell, side[1, i] * is_last_col, 0) == 1
        first[low + i, :, at:chunk] = jnp.where(
            mark, ground[low + i, :, at:chunk], first[low + i, :, at:chunk]
        )
        for number, ref in enumerate((first, ground)):
            ring = ring_of(ref, low + i)
            ring_own[number, i] = ring
            ref[low + i, :, chunk:lanes] = ring

    order = [i for i in range(height) if i < DEPTH or i >= height - DEPTH]
    order += [i for i in range(height) if i not in order]
    for i in order:
        start_row(i)

    pl.semaphore_wait(barrier, members - 1)

    copies = []

    def send(src, dst, dr, dc):
        number = len(copies)
        copy = pltpu.make_async_remote_copy(
            src_ref=src,
            dst_ref=dst,
            send_sem=send_sem.at[number],
            recv_sem=recv_sem.at[number],
            device_id=device(dr, dc),
            device_id_type=MESH,
        )
        pl.when(both(dr, dc))(copy.start)
        copies.append((copy, dr, dc))
        return copy, dr, dc

    def arrive(entry):
        copy, dr, dc = entry
        pl.when(both(-dr, -dc))(copy.wait_recv)

    def rows_out(ref, dr, extent):
        src = low if dr == -1 else high - DEPTH
        dst = high if dr == -1 else 0
        return send(
            ref.at[pl.ds(src, DEPTH), :, pl.ds(0, extent)],
            ref.at[pl.ds(dst, DEPTH), :, pl.ds(0, extent)],
            dr, 0,
        )

    ring_in = []
    for dc in (-1, 1):
        for dr in (-1, 0, 1):
            at, count = {-1: (0, DEPTH), 0: (0, height), 1: (height - DEPTH, DEPTH)}[dr]
            to, _ = spans[-dr]
            target = ring_high if dc == -1 else ring_low
            part = SUBL - 1 if dc == -1 else 0
            ring_in.append(
                send(
                    ring_own.at[:, pl.ds(at, count), pl.ds(part, 1)],
                    target.at[:, pl.ds(to, count)],
                    dr, dc,
                )
            )
    row_in = {dr: [] for dr in (-1, 1)}
    for ref in (first, ground):
        for dr in (-1, 1):
            row_in[-dr].append(rows_out(ref, dr, chunk))

    def relax_rows(src, dst, r, count):
        rows = [src[r - 1 + i] for i in range(count + 2)]
        for i in range(count):
            above, here, below = rows[i : i + 3]
            low3 = jnp.minimum(jnp.minimum(above, below), here)
            least = jnp.minimum(
                low3, jnp.minimum(pltpu.roll(low3, 1, 1), pltpu.roll(low3, lanes - 1, 1))
            )
            value = jnp.maximum(ground[r + i], jnp.minimum(here, least + rise_step))
            if dst is done:
                done[r + i - low] = value[:, 0:chunk]
            else:
                dst[r + i] = value

    def inner(chain):
        for k in range(1, DEPTH + 1):
            src, dst = chain[k - 1], chain[k]
            begin, end = low + k, high - k

            def body(step, carry, src=src, dst=dst, begin=begin):
                relax_rows(src, dst, begin + 2 * step, 2)
                return carry

            lax.fori_loop(0, (end - begin) // 2, body, 0)

    def outer(chain, dr):
        for k in range(1, DEPTH + 1):
            begin = k if dr == -1 else high - k
            for i in range(0, DEPTH, 2):
                relax_rows(chain[k - 1], chain[k], begin + i, 2)

    def finish_ring(at, count):
        for r in range(at, at + count):
            for number, ref in enumerate((first, ground)):
                if at == low:
                    ring = ring_own[number, r - low]
                else:
                    ring = ring_of(ref, r)
                from_high = jnp.broadcast_to(ring_high[number, r], (SUBL, TILE))
                from_low = jnp.broadcast_to(ring_low[number, r], (SUBL, TILE))
                ring = jnp.where(
                    jnp.logical_and(sub_id == SUBL - 1, right_half), from_high, ring
                )
                ring = jnp.where(
                    jnp.logical_and(sub_id == 0, jnp.logical_not(right_half)), from_low, ring
                )
                ref[r, :, chunk:lanes] = ring

    for entry in ring_in:
        arrive(entry)
    finish_ring(low, height)
    chain = (first, ping, pong, ping, second)
    inner(chain)
    for dr, at in ((-1, 0), (1, high)):
        for entry in row_in[dr]:
            arrive(entry)
        finish_ring(at, DEPTH)
        outer(chain, dr)

    row_in = {-dr: rows_out(second, dr, lanes) for dr in (-1, 1)}
    chain = (second, ping, pong, ping, third)
    inner(chain)
    for dr in (-1, 1):
        arrive(row_in[dr])
        outer(chain, dr)

    row_in = {-dr: rows_out(third, dr, lanes) for dr in (-1, 1)}
    first_tile = third[low, :, 0:TILE]
    last_tile = third[low, :, chunk - TILE : chunk]
    for i in range(1, height):
        first_tile = jnp.minimum(first_tile, third[low + i, :, 0:TILE])
        last_tile = jnp.minimum(last_tile, third[low + i, :, chunk - TILE : chunk])
    floor = jnp.minimum(
        jnp.where(first_cell, first_tile, unreached), jnp.where(last_cell, last_tile, unreached)
    )
    for i, counts in ((low, sub == 0), (high - 1, sub == n_sub - 1)):
        skip = jnp.where(counts, -unreached, unreached)
        for j in range(chunk // TILE):
            floor = jnp.minimum(
                floor, jnp.maximum(third[i, :, j * TILE : (j + 1) * TILE], skip)
            )
    floor = jnp.min(floor, axis=(0, 1), keepdims=True)
    tile_id = tile_row * n_cols + col
    mine[...] = jnp.where(
        lax.broadcasted_iota(jnp.int32, (1, padded), 1) == tile_id,
        jnp.broadcast_to(floor, (1, padded)),
        unreached,
    )

    def level_copy(step):
        return pltpu.make_async_remote_copy(
            src_ref=mine,
            dst_ref=gathered.at[members - 1 - step],
            send_sem=level_send,
            recv_sem=level_recv,
            device_id=member((me + step) % members),
            device_id_type=MESH,
        )

    def spread(step, carry):
        level_copy(step).start()
        return carry

    lax.fori_loop(1, members, spread, 0)
    pltpu.make_async_copy(gathered, gathered, level_recv).wait()
    row = jnp.minimum(mine[...], jnp.min(gathered[...], axis=0))
    count = hops[...]
    best = jnp.full((n_tiles, padded), unreached, jnp.float32)
    for step in range(ROUNDS + 1):
        best = jnp.minimum(
            best, jnp.where(count == float(step), jnp.broadcast_to(row, best.shape), unreached)
        )
        row = row + hop_rise
    level = jnp.min(best, axis=1, keepdims=True)
    levels[...] = jnp.broadcast_to(level + spill_lift, levels.shape)

    def ceiling(row_at, col_at):
        at = jnp.clip(row_at, 0, n_rows - 1) * n_cols + jnp.clip(col_at, 0, n_cols - 1)
        return jnp.broadcast_to(levels[pl.ds(at, 1)], (SUBL, TILE))

    def clamp(at, count, row_at):
        here = ceiling(row_at, col)
        ring = jnp.where(
            jnp.logical_and(sub_id == SUBL - 1, right_half), ceiling(row_at, col + 1), here
        )
        ring = jnp.where(
            jnp.logical_and(sub_id == 0, jnp.logical_not(right_half)), ceiling(row_at, col - 1), ring
        )
        for r in range(at, at + count):
            for j in range(lanes // TILE):
                cut = slice(j * TILE, (j + 1) * TILE)
                top = ring if j == lanes // TILE - 1 else here
                pong[r, :, cut] = jnp.maximum(
                    ground[r, :, cut], jnp.minimum(third[r, :, cut], top)
                )

    clamp(low, height, tile_row)
    chain = (pong, ping, pong, ping, done)
    inner(chain)
    for dr, at in ((-1, 0), (1, high)):
        arrive(row_in[dr])
        clamp(at, DEPTH, (band + dr + n_sub) // n_sub - 1)
        outer(chain, dr)

    for s in range(SUBL):
        pltpu.make_async_copy(
            done.at[:, s], out_hbm.at[:, pl.ds(s * chunk, chunk)], out_sem
        ).start()
    for copy, dr, dc in copies:
        pl.when(both(dr, dc))(copy.wait_send)
    pltpu.make_async_copy(gathered, gathered, level_send).wait()
    pltpu.make_async_copy(done, done, out_sem).wait()


def per_device(sizes, elevation, fill_depth, edge_rows, edge_sides, adjacency):
    height, width = elevation.shape
    chunk = width // SUBL
    total = height + 2 * DEPTH
    members = sizes[1] * sizes[2] * sizes[3]
    n_tiles = adjacency.shape[0]
    padded = -(-n_tiles // TILE) * TILE
    wide = pltpu.VMEM((total, SUBL, chunk + TILE), jnp.float32)
    own = pltpu.VMEM((height, SUBL, chunk), jnp.float32)
    ring = pltpu.VMEM((2, total, 1, TILE), jnp.float32)
    return pl.pallas_call(
        functools.partial(kernel, sizes),
        out_shape=jax.ShapeDtypeStruct((height, width), jnp.float32),
        in_specs=[pl.BlockSpec(memory_space=pl.ANY)] * 5,
        out_specs=pl.BlockSpec(memory_space=pl.ANY),
        scratch_shapes=[
            wide, own, wide, wide, wide, wide, wide, own,
            pltpu.VMEM((2, SUBL, chunk), jnp.int32),
            pltpu.SMEM(edge_sides.shape, jnp.int32),
            pltpu.VMEM(adjacency.shape, jnp.int32),
            pltpu.VMEM((2, height, SUBL, TILE), jnp.float32),
            ring, ring,
            pltpu.VMEM((1, padded), jnp.float32),
            pltpu.VMEM((members - 1, 1, padded), jnp.float32),
            pltpu.VMEM((n_tiles, padded), jnp.float32),
            pltpu.VMEM((n_tiles, TILE), jnp.float32),
            pltpu.SemaphoreType.DMA((5,)),
            pltpu.SemaphoreType.DMA((14,)),
            pltpu.SemaphoreType.DMA((14,)),
            pltpu.SemaphoreType.DMA,
            pltpu.SemaphoreType.DMA,
            pltpu.SemaphoreType.DMA,
        ],
        compiler_params=pltpu.CompilerParams(
            collective_id=0, has_side_effects=True, vmem_limit_bytes=32 * 1024 * 1024
        ),
    )(elevation, fill_depth, edge_rows, edge_sides, adjacency)


def solution(mesh):
    sizes = tuple(mesh.shape[name] for name in ("groups", "rows", "cols", "sub"))
    placed = (
        P(("groups", "rows", "sub"), "cols"),
        P(("groups", "rows", "sub"), "cols"),
        P("groups", "cols"),
        P("groups", ("rows", "sub")),
        P("groups", None),
    )
    return jax.shard_map(
        functools.partial(per_device, sizes),
        mesh=mesh,
        in_specs=placed,
        out_specs=P(("groups", "rows", "sub"), "cols"),
        check_vma=False,
    )
```

```python
import functools

import jax
import jax.numpy as jnp
from jax import lax
from jax.experimental import pallas as pl
from jax.experimental.pallas import tpu as pltpu
from jax.sharding import PartitionSpec as P

PASSES = 8
ROUNDS = 4

unreached = 1000000000.0
rise_step = 0.01
hop_rise = 0.05
spill_lift = 3.0

DEPTH = 4
SUBL = 8
TILE = 128
HALF = TILE // 2
MESH = pl.DeviceIdType.MESH


def kernel(
    sizes, elev_hbm, fill_hbm, edge_hbm, side_hbm, adj_hbm, out_hbm,
    ground, fill, first, second, third, ping, pong, done,
    edge, side, adj, ring_own, ring_low, ring_high,
    mine, gathered, hops, levels, even, odd, seam_ground,
    load_sem, send_sem, recv_sem, level_send, level_recv, out_sem,
):
    n_groups, n_rows, n_cols, n_sub = sizes
    height, width = elev_hbm.shape
    chunk = width // SUBL
    lanes = chunk + TILE
    low, high = DEPTH, DEPTH + height
    total = height + 2 * DEPTH
    n_tiles = adj.shape[0]
    padded = mine.shape[1]
    members = n_rows * n_cols * n_sub

    group = lax.axis_index("groups")
    tile_row = lax.axis_index("rows")
    col = lax.axis_index("cols")
    sub = lax.axis_index("sub")
    band = tile_row * n_sub + sub
    bands = n_rows * n_sub
    me = (tile_row * n_cols + col) * n_sub + sub

    near = 1 - 2 * (band % 2)
    far = -near

    def has(dr):
        return jnp.logical_and(band + dr >= 0, band + dr < bands)

    has_col = {-1: col > 0, 1: col < n_cols - 1}

    def both(dr, dc):
        if dc == 0:
            return has(dr)
        if isinstance(dr, int) and dr == 0:
            return has_col[dc]
        return jnp.logical_and(has(dr), has_col[dc])

    def device(dr, dc):
        to_band = band + dr
        return (group, to_band // n_sub, col + dc, to_band % n_sub)

    barrier = pltpu.get_barrier_semaphore()

    def member(number):
        return (group, number // (n_sub * n_cols), (number // n_sub) % n_cols, number % n_sub)

    def greet(step, carry):
        pl.semaphore_signal(
            barrier, inc=1, device_id=member((me + step) % members), device_id_type=MESH
        )
        return carry

    lax.fori_loop(1, members, greet, 0)

    loads = []
    for number, (src, dst, at) in enumerate(
        ((elev_hbm, ground, low), (fill_hbm, fill, 0), (edge_hbm, edge, 0))
    ):
        count = src.shape[0]
        for s in range(SUBL):
            pltpu.make_async_copy(
                src.at[:, pl.ds(s * chunk, chunk)],
                dst.at[pl.ds(at, count), s, pl.ds(0, chunk)],
                load_sem.at[number],
            ).start()
        whole = dst.at[pl.ds(at, count), :, pl.ds(0, chunk)]
        loads.append(pltpu.make_async_copy(whole, whole, load_sem.at[number]))
    side_load = pltpu.make_async_copy(side_hbm, side, load_sem.at[3])
    side_load.start()
    adj_load = pltpu.make_async_copy(adj_hbm, adj, load_sem.at[4])
    adj_load.start()

    def outside_rows(at):
        for ref in (ground, first, second, third):
            ref[pl.ds(at, DEPTH)] = jnp.full((DEPTH, SUBL, lanes), unreached, jnp.float32)

    pl.when(jnp.logical_not(has(-1)))(lambda: outside_rows(0))
    pl.when(jnp.logical_not(has(1)))(lambda: outside_rows(high))

    spans = {-1: (0, DEPTH), 0: (low, height), 1: (high, DEPTH)}
    for dc, ref in ((-1, ring_low), (1, ring_high)):
        for dr in (-1, 0, 1):

            def outside_ring(ref=ref, dr=dr):
                at, count = spans[dr]
                ref[:, pl.ds(at, count)] = jnp.full((2, count, 1, TILE), unreached, jnp.float32)

            pl.when(jnp.logical_not(both(dr, dc)))(outside_ring)

    adj_load.wait()
    lane_tile = lax.broadcasted_iota(jnp.int32, (n_tiles, padded), 1)
    linked = jnp.zeros((n_tiles, padded), jnp.float32)
    links = adj[...]
    for k in range(links.shape[1]):
        linked = jnp.where(links[:, k : k + 1] == lane_tile, 1.0, linked)
    own = lax.broadcasted_iota(jnp.int32, (n_tiles, padded), 0) == lane_tile
    linked = jnp.where(own, 1.0, linked)
    one_hop = linked
    if n_tiles < padded:
        one_hop = jnp.concatenate(
            [one_hop, jnp.zeros((padded - n_tiles, padded), jnp.float32)], axis=0
        )
    count = jnp.where(own, 0.0, 1.0)
    reach = linked
    for step in range(ROUNDS):
        count = count + (1.0 - reach)
        if step < ROUNDS - 1:
            reach = jnp.dot(reach, one_hop, preferred_element_type=jnp.float32)
            reach = jnp.where(reach > 0.5, 1.0, 0.0)
    hops[...] = count

    sub_id = lax.broadcasted_iota(jnp.int32, (SUBL, TILE), 0)
    lane_id = lax.broadcasted_iota(jnp.int32, (SUBL, TILE), 1)
    first_cell = jnp.logical_and(sub_id == 0, lane_id == 0)
    last_cell = jnp.logical_and(sub_id == SUBL - 1, lane_id == TILE - 1)
    is_first_col = (col == 0).astype(jnp.int32)
    is_last_col = (col == n_cols - 1).astype(jnp.int32)
    top_mark = jnp.where(band == 0, 1, 2)
    bottom_mark = jnp.where(band == bands - 1, 1, 2)
    right_half = lane_id < HALF

    def ring_of(ref, r):
        left_tile = ref[r, :, 0:TILE]
        right_tile = ref[r, :, chunk - TILE : chunk]
        return jnp.where(
            right_half, pltpu.roll(left_tile, SUBL - 1, 0), pltpu.roll(right_tile, 1, 0)
        )

    side_load.wait()
    for load in loads:
        load.wait()

    def start_row(i):
        height_row = ground[low + i, :, 0:chunk]
        water = height_row + fill[i]
        if i == 0:
            water = jnp.where(edge[0] == top_mark, height_row, water)
        if i == height - 1:
            water = jnp.where(edge[1] == bottom_mark, height_row, water)
        first[low + i, :, 0:chunk] = water
        mark = jnp.where(first_cell, side[0, i] * is_first_col, 0) == 1
        first[low + i, :, 0:TILE] = jnp.where(
            mark, ground[low + i, :, 0:TILE], first[low + i, :, 0:TILE]
        )
        at = chunk - TILE
        mark = jnp.where(last_cell, side[1, i] * is_last_col, 0) == 1
        first[low + i, :, at:chunk] = jnp.where(
            mark, ground[low + i, :, at:chunk], first[low + i, :, at:chunk]
        )
        for number, ref in enumerate((first, ground)):
            ring = ring_of(ref, low + i)
            ring_own[number, i] = ring
            ref[low + i, :, chunk:lanes] = ring

    order = [i for i in range(height) if i < DEPTH or i >= height - DEPTH]
    order += [i for i in range(height) if i not in order]
    for i in order:
        start_row(i)

    pl.semaphore_wait(barrier, members - 1)

    copies = []

    def send(src, dst, dr, dc):
        number = len(copies)
        copy = pltpu.make_async_remote_copy(
            src_ref=src,
            dst_ref=dst,
            send_sem=send_sem.at[number],
            recv_sem=recv_sem.at[number],
            device_id=device(dr, dc),
            device_id_type=MESH,
        )
        pl.when(both(dr, dc))(copy.start)
        copies.append((copy, dr, dc))
        return copy, dr, dc

    def arrive(entry, mirrored):
        copy, dr, dc = entry
        pl.when(both(-dr, -dc) if mirrored else both(dr, dc))(copy.wait_recv)

    def rows_out(ref, dr, extent):
        src = jnp.where(dr < 0, low, high - DEPTH)
        dst = jnp.where(dr < 0, high, 0)
        return send(
            ref.at[pl.ds(src, DEPTH), :, pl.ds(0, extent)],
            ref.at[pl.ds(dst, DEPTH), :, pl.ds(0, extent)],
            dr, 0,
        )

    ring_in = []
    for dc in (-1, 1):
        for dr in (-1, 0, 1):
            at, count = {-1: (0, DEPTH), 0: (0, height), 1: (height - DEPTH, DEPTH)}[dr]
            to, _ = spans[-dr]
            target = ring_high if dc == -1 else ring_low
            part = SUBL - 1 if dc == -1 else 0
            ring_in.append(
                send(
                    ring_own.at[:, pl.ds(at, count), pl.ds(part, 1)],
                    target.at[:, pl.ds(to, count)],
                    dr, dc,
                )
            )
    sides = (near, far)
    row_in = [[rows_out(ref, dr, chunk) for ref in (first, ground)] for dr in sides]

    def relax_rows(src, dst, r, count):
        rows = [src[r - 1 + i] for i in range(count + 2)]
        for i in range(count):
            above, here, below = rows[i : i + 3]
            low3 = jnp.minimum(jnp.minimum(above, below), here)
            least = jnp.minimum(
                low3, jnp.minimum(pltpu.roll(low3, 1, 1), pltpu.roll(low3, lanes - 1, 1))
            )
            value = jnp.maximum(ground[r + i], jnp.minimum(here, least + rise_step))
            if dst is done:
                done[r + i - low] = value[:, 0:chunk]
            else:
                dst[r + i] = value

    def inner(chain):
        for k in range(1, DEPTH + 1):
            for r in range(low + k, high - k, 2):
                relax_rows(chain[k - 1], chain[k], r, 2)

    def outer(chain, dr):
        for k in range(1, DEPTH + 1):
            begin = jnp.where(dr < 0, k, high - k)
            for i in range(0, DEPTH, 2):
                relax_rows(chain[k - 1], chain[k], begin + i, 2)

    def finish_ring(at, count, own_rows):
        for i in range(count):
            r = at + i
            for number, ref in enumerate((first, ground)):
                ring = ring_own[number, i] if own_rows else ring_of(ref, r)
                from_high = jnp.broadcast_to(ring_high[number, r], (SUBL, TILE))
                from_low = jnp.broadcast_to(ring_low[number, r], (SUBL, TILE))
                ring = jnp.where(at_high, from_high, jnp.where(at_low, from_low, ring))
                ref[r, :, chunk:lanes] = ring

    at_high = jnp.logical_and(sub_id == SUBL - 1, right_half)
    at_low = jnp.logical_and(sub_id == 0, jnp.logical_not(right_half))

    for entry in ring_in:
        arrive(entry, True)
    finish_ring(low, height, True)
    chain = (first, ping, pong, ping, second)
    inner(chain)
    row_next = []
    for dr, entries in zip(sides, row_in):
        for entry in entries:
            arrive(entry, False)
        finish_ring(jnp.where(dr < 0, 0, high), DEPTH, False)
        outer(chain, dr)
        row_next.append(rows_out(second, dr, lanes))

    row_in = row_next
    chain = (second, ping, pong, ping, third)
    inner(chain)
    for dr, entry in zip(sides, row_in):
        arrive(entry, False)
        outer(chain, dr)

    first_tile = third[low, :, 0:TILE]
    last_tile = third[low, :, chunk - TILE : chunk]
    for i in range(1, height):
        first_tile = jnp.minimum(first_tile, third[low + i, :, 0:TILE])
        last_tile = jnp.minimum(last_tile, third[low + i, :, chunk - TILE : chunk])
    floor = jnp.minimum(
        jnp.where(first_cell, first_tile, unreached), jnp.where(last_cell, last_tile, unreached)
    )
    for i, counts in ((low, sub == 0), (high - 1, sub == n_sub - 1)):
        skip = jnp.where(counts, -unreached, unreached)
        for j in range(chunk // TILE):
            floor = jnp.minimum(
                floor, jnp.maximum(third[i, :, j * TILE : (j + 1) * TILE], skip)
            )
    floor = jnp.min(floor, axis=(0, 1), keepdims=True)
    tile_id = tile_row * n_cols + col
    mine[...] = jnp.where(
        lax.broadcasted_iota(jnp.int32, (1, padded), 1) == tile_id,
        jnp.broadcast_to(floor, (1, padded)),
        unreached,
    )

    def level_copy(step):
        return pltpu.make_async_remote_copy(
            src_ref=mine,
            dst_ref=gathered.at[members - 1 - step],
            send_sem=level_send,
            recv_sem=level_recv,
            device_id=member((me + step) % members),
            device_id_type=MESH,
        )

    def spread(step, carry):
        level_copy(step).start()
        return carry

    lax.fori_loop(1, members, spread, 0)
    row_in = [rows_out(third, dr, lanes) for dr in (far, near)][::-1]

    chain = (third, ping, pong, ping, done)
    inner(chain)
    for dr, entry in zip(sides, row_in):
        arrive(entry, False)
        outer(chain, dr)

    def seam_of(ref, r):
        ring = ref[r, :, chunk:lanes]
        at_first = jnp.where(right_half, ref[r, :, 0:TILE], ring)
        at_last = jnp.where(right_half, ring, ref[r, :, chunk - TILE : chunk])
        return jnp.where(sub_id == 0, at_first, at_last)

    for r in range(total):
        seam_ground[r] = seam_of(ground, r)

    pltpu.make_async_copy(gathered, gathered, level_recv).wait()
    row = jnp.minimum(mine[...], jnp.min(gathered[...], axis=0))
    count = hops[...]
    best = jnp.full((n_tiles, padded), unreached, jnp.float32)
    for step in range(ROUNDS + 1):
        best = jnp.minimum(
            best, jnp.where(count == float(step), jnp.broadcast_to(row, best.shape), unreached)
        )
        row = row + hop_rise
    level = jnp.min(best, axis=1, keepdims=True)
    levels[...] = jnp.broadcast_to(level + spill_lift, levels.shape)

    def ceiling(row_at, col_at):
        at = jnp.clip(row_at, 0, n_rows - 1) * n_cols + jnp.clip(col_at, 0, n_cols - 1)
        return jnp.broadcast_to(levels[pl.ds(at, 1)], (SUBL, TILE))

    def ceilings(row_at):
        here = ceiling(row_at, col)
        beside = jnp.where(
            at_high, ceiling(row_at, col + 1), jnp.where(at_low, ceiling(row_at, col - 1), here)
        )
        return here, beside

    above, own_row, below = (ceilings((band + dr + n_sub) // n_sub - 1) for dr in (-1, 0, 1))
    beyond = ceilings((band + far + n_sub) // n_sub - 1)

    seam = []
    for r in range(total):
        top = (above if r < low else own_row if r < high else below)[1]
        seam.append(jnp.maximum(seam_ground[r], top))
    for k in range(1, DEPTH + 1):
        later = list(seam)
        for r in range(k, total - k):
            low3 = jnp.minimum(jnp.minimum(seam[r - 1], seam[r + 1]), seam[r])
            least = jnp.minimum(
                low3, jnp.minimum(pltpu.roll(low3, 1, 1), pltpu.roll(low3, TILE - 1, 1))
            )
            later[r] = jnp.maximum(seam_ground[r], jnp.minimum(seam[r], least + rise_step))
        seam = later
    for i in range(height):
        seam_ground[low + i] = seam[low + i]

    def flat(at, count, tops, targets):
        here, beside = tops
        for i in range(count):
            for j in range(lanes // TILE):
                cut = slice(j * TILE, (j + 1) * TILE)
                top = beside if j == lanes // TILE - 1 else here
                value = jnp.maximum(ground[at + i, :, cut], top)
                for target in targets:
                    target[at + i, :, cut] = value

    flat(jnp.where(far < 0, 0, high), DEPTH, beyond, (even,))
    flat(jnp.where(far < 0, low, high - DEPTH - 1), DEPTH + 1, own_row, (even, odd))
    outer((even, odd, even, odd, even), far)

    left_seam = jnp.logical_and(sub_id == 0, lane_id < DEPTH)
    right_seam = jnp.logical_and(sub_id == SUBL - 1, lane_id >= TILE - DEPTH)

    def merge(at, count, is_far):
        for i in range(count):
            r = at + i
            for j in range(chunk // TILE):
                cut = slice(j * TILE, (j + 1) * TILE)
                top = even[r, :, cut] if is_far else jnp.maximum(ground[r, :, cut], own_row[0])
                value = jnp.minimum(done[r - low, :, cut], top)
                if j == 0:
                    value = jnp.where(left_seam, jnp.minimum(value, seam_ground[r]), value)
                if j == chunk // TILE - 1:
                    value = jnp.where(right_seam, jnp.minimum(value, seam_ground[r]), value)
                done[r - low, :, cut] = value

    merge(jnp.where(far < 0, low + DEPTH, low), height - DEPTH, False)
    merge(jnp.where(far < 0, low, high - DEPTH), DEPTH, True)

    for s in range(SUBL):
        pltpu.make_async_copy(
            done.at[:, s], out_hbm.at[:, pl.ds(s * chunk, chunk)], out_sem
        ).start()
    for copy, dr, dc in copies:
        pl.when(both(dr, dc))(copy.wait_send)
    pltpu.make_async_copy(gathered, gathered, level_send).wait()
    pltpu.make_async_copy(done, done, out_sem).wait()


def per_device(sizes, elevation, fill_depth, edge_rows, edge_sides, adjacency):
    height, width = elevation.shape
    chunk = width // SUBL
    total = height + 2 * DEPTH
    members = sizes[1] * sizes[2] * sizes[3]
    n_tiles = adjacency.shape[0]
    padded = -(-n_tiles // TILE) * TILE
    wide = pltpu.VMEM((total, SUBL, chunk + TILE), jnp.float32)
    own = pltpu.VMEM((height, SUBL, chunk), jnp.float32)
    ring = pltpu.VMEM((2, total, 1, TILE), jnp.float32)
    return pl.pallas_call(
        functools.partial(kernel, sizes),
        out_shape=jax.ShapeDtypeStruct((height, width), jnp.float32),
        in_specs=[pl.BlockSpec(memory_space=pltpu.HBM)] * 5,
        out_specs=pl.BlockSpec(memory_space=pl.ANY),
        scratch_shapes=[
            wide, own, wide, wide, wide, wide, wide, own,
            pltpu.VMEM((2, SUBL, chunk), jnp.int32),
            pltpu.SMEM(edge_sides.shape, jnp.int32),
            pltpu.VMEM(adjacency.shape, jnp.int32),
            pltpu.VMEM((2, height, SUBL, TILE), jnp.float32),
            ring, ring,
            pltpu.VMEM((1, padded), jnp.float32),
            pltpu.VMEM((members - 1, 1, padded), jnp.float32),
            pltpu.VMEM((n_tiles, padded), jnp.float32),
            pltpu.VMEM((n_tiles, TILE), jnp.float32),
            wide, wide,
            pltpu.VMEM((total, SUBL, TILE), jnp.float32),
            pltpu.SemaphoreType.DMA((5,)),
            pltpu.SemaphoreType.DMA((14,)),
            pltpu.SemaphoreType.DMA((14,)),
            pltpu.SemaphoreType.DMA,
            pltpu.SemaphoreType.DMA,
            pltpu.SemaphoreType.DMA,
        ],
        compiler_params=pltpu.CompilerParams(
            collective_id=0, has_side_effects=True, vmem_limit_bytes=32 * 1024 * 1024
        ),
    )(elevation, fill_depth, edge_rows, edge_sides, adjacency)


def solution(mesh):
    sizes = tuple(mesh.shape[name] for name in ("groups", "rows", "cols", "sub"))
    placed = (
        P(("groups", "rows", "sub"), "cols"),
        P(("groups", "rows", "sub"), "cols"),
        P("groups", "cols"),
        P("groups", ("rows", "sub")),
        P("groups", None),
    )
    return jax.shard_map(
        functools.partial(per_device, sizes),
        mesh=mesh,
        in_specs=placed,
        out_specs=P(("groups", "rows", "sub"), "cols"),
        check_vma=False,
    )
```

```python
import functools

import jax
import jax.numpy as jnp
from jax import lax
from jax.experimental import pallas as pl
from jax.experimental.pallas import tpu as pltpu
from jax.sharding import PartitionSpec as P

PASSES = 8
ROUNDS = 4

unreached = 1000000000.0
rise_step = 0.01
hop_rise = 0.05
spill_lift = 3.0

DEPTH = 4
SUBL = 8
TILE = 128
HALF = TILE // 2
MESH = pl.DeviceIdType.MESH


def kernel(
    sizes, elev_hbm, fill_hbm, edge_hbm, side_hbm, adj_hbm, out_hbm,
    ground, fill, first, second, third, ping, pong, done,
    edge, side, adj, ring_own, ring_low, ring_high,
    mine, gathered, hops, levels, even, odd, seam_ground,
    load_sem, send_sem, recv_sem, level_send, level_recv, out_sem,
):
    n_groups, n_rows, n_cols, n_sub = sizes
    height, width = elev_hbm.shape
    chunk = width // SUBL
    lanes = chunk + TILE
    low, high = DEPTH, DEPTH + height
    total = height + 2 * DEPTH
    n_tiles = adj.shape[0]
    padded = mine.shape[1]
    members = n_rows * n_cols * n_sub

    group = lax.axis_index("groups")
    tile_row = lax.axis_index("rows")
    col = lax.axis_index("cols")
    sub = lax.axis_index("sub")
    band = tile_row * n_sub + sub
    bands = n_rows * n_sub
    me = (tile_row * n_cols + col) * n_sub + sub

    near = 1 - 2 * (band % 2)
    far = -near

    def has(dr):
        return jnp.logical_and(band + dr >= 0, band + dr < bands)

    has_col = {-1: col > 0, 1: col < n_cols - 1}

    def both(dr, dc):
        if dc == 0:
            return has(dr)
        if isinstance(dr, int) and dr == 0:
            return has_col[dc]
        return jnp.logical_and(has(dr), has_col[dc])

    def device(dr, dc):
        to_band = band + dr
        return (group, to_band // n_sub, col + dc, to_band % n_sub)

    barrier = pltpu.get_barrier_semaphore()

    def member(number):
        return (group, number // (n_sub * n_cols), (number // n_sub) % n_cols, number % n_sub)

    def greet(step, carry):
        pl.semaphore_signal(
            barrier, inc=1, device_id=member((me + step) % members), device_id_type=MESH
        )
        return carry

    lax.fori_loop(1, members, greet, 0)

    loads = []
    for number, (src, dst, at) in enumerate(
        ((elev_hbm, ground, low), (fill_hbm, fill, 0), (edge_hbm, edge, 0))
    ):
        count = src.shape[0]
        for s in range(SUBL):
            pltpu.make_async_copy(
                src.at[:, pl.ds(s * chunk, chunk)],
                dst.at[pl.ds(at, count), s, pl.ds(0, chunk)],
                load_sem.at[number],
            ).start()
        whole = dst.at[pl.ds(at, count), :, pl.ds(0, chunk)]
        loads.append(pltpu.make_async_copy(whole, whole, load_sem.at[number]))
    side_load = pltpu.make_async_copy(side_hbm, side, load_sem.at[3])
    side_load.start()
    adj_load = pltpu.make_async_copy(adj_hbm, adj, load_sem.at[4])
    adj_load.start()

    def outside_rows(at):
        for ref in (ground, first, second, third):
            ref[pl.ds(at, DEPTH)] = jnp.full((DEPTH, SUBL, lanes), unreached, jnp.float32)

    pl.when(jnp.logical_not(has(-1)))(lambda: outside_rows(0))
    pl.when(jnp.logical_not(has(1)))(lambda: outside_rows(high))

    spans = {-1: (0, DEPTH), 0: (low, height), 1: (high, DEPTH)}
    for dc, ref in ((-1, ring_low), (1, ring_high)):
        for dr in (-1, 0, 1):

            def outside_ring(ref=ref, dr=dr):
                at, count = spans[dr]
                ref[:, pl.ds(at, count)] = jnp.full((2, count, 1, TILE), unreached, jnp.float32)

            pl.when(jnp.logical_not(both(dr, dc)))(outside_ring)

    sub_id = lax.broadcasted_iota(jnp.int32, (SUBL, TILE), 0)
    lane_id = lax.broadcasted_iota(jnp.int32, (SUBL, TILE), 1)
    first_cell = jnp.logical_and(sub_id == 0, lane_id == 0)
    last_cell = jnp.logical_and(sub_id == SUBL - 1, lane_id == TILE - 1)
    is_first_col = (col == 0).astype(jnp.int32)
    is_last_col = (col == n_cols - 1).astype(jnp.int32)
    top_mark = jnp.where(band == 0, 1, 2)
    bottom_mark = jnp.where(band == bands - 1, 1, 2)
    right_half = lane_id < HALF

    def ring_of(ref, r):
        left_tile = ref[r, :, 0:TILE]
        right_tile = ref[r, :, chunk - TILE : chunk]
        return jnp.where(
            right_half, pltpu.roll(left_tile, SUBL - 1, 0), pltpu.roll(right_tile, 1, 0)
        )

    side_load.wait()
    for load in loads:
        load.wait()

    def start_row(i):
        height_row = ground[low + i, :, 0:chunk]
        water = height_row + fill[i]
        if i == 0:
            water = jnp.where(edge[0] == top_mark, height_row, water)
        if i == height - 1:
            water = jnp.where(edge[1] == bottom_mark, height_row, water)
        first[low + i, :, 0:chunk] = water
        mark = jnp.where(first_cell, side[0, i] * is_first_col, 0) == 1
        first[low + i, :, 0:TILE] = jnp.where(
            mark, ground[low + i, :, 0:TILE], first[low + i, :, 0:TILE]
        )
        at = chunk - TILE
        mark = jnp.where(last_cell, side[1, i] * is_last_col, 0) == 1
        first[low + i, :, at:chunk] = jnp.where(
            mark, ground[low + i, :, at:chunk], first[low + i, :, at:chunk]
        )
        for number, ref in enumerate((first, ground)):
            ring = ring_of(ref, low + i)
            ring_own[number, i] = ring
            ref[low + i, :, chunk:lanes] = ring

    order = [i for i in range(height) if i < DEPTH or i >= height - DEPTH]
    order += [i for i in range(height) if i not in order]
    for i in order:
        start_row(i)

    pl.semaphore_wait(barrier, members - 1)

    copies = []

    def send(src, dst, dr, dc):
        number = len(copies)
        copy = pltpu.make_async_remote_copy(
            src_ref=src,
            dst_ref=dst,
            send_sem=send_sem.at[number],
            recv_sem=recv_sem.at[number],
            device_id=device(dr, dc),
            device_id_type=MESH,
        )
        pl.when(both(dr, dc))(copy.start)
        copies.append((copy, dr, dc))
        return copy, dr, dc

    def arrive(entry, mirrored):
        copy, dr, dc = entry
        pl.when(both(-dr, -dc) if mirrored else both(dr, dc))(copy.wait_recv)

    def rows_out(ref, dr, extent):
        src = jnp.where(dr < 0, low, high - DEPTH)
        dst = jnp.where(dr < 0, high, 0)
        return send(
            ref.at[pl.ds(src, DEPTH), :, pl.ds(0, extent)],
            ref.at[pl.ds(dst, DEPTH), :, pl.ds(0, extent)],
            dr, 0,
        )

    ring_in = []
    for dc in (-1, 1):
        for dr in (-1, 0, 1):
            at, count = {-1: (0, DEPTH), 0: (0, height), 1: (height - DEPTH, DEPTH)}[dr]
            to, _ = spans[-dr]
            target = ring_high if dc == -1 else ring_low
            part = SUBL - 1 if dc == -1 else 0
            ring_in.append(
                send(
                    ring_own.at[:, pl.ds(at, count), pl.ds(part, 1)],
                    target.at[:, pl.ds(to, count)],
                    dr, dc,
                )
            )
    sides = (near, far)
    row_in = [[rows_out(ref, dr, chunk) for ref in (first, ground)] for dr in sides]

    def relax_rows(src, dst, r, count):
        rows = [src[r - 1 + i] for i in range(count + 2)]
        for i in range(count):
            above, here, below = rows[i : i + 3]
            low3 = jnp.minimum(jnp.minimum(above, below), here)
            least = jnp.minimum(
                low3, jnp.minimum(pltpu.roll(low3, 1, 1), pltpu.roll(low3, lanes - 1, 1))
            )
            value = jnp.maximum(ground[r + i], jnp.minimum(here, least + rise_step))
            if dst is done:
                done[r + i - low] = value[:, 0:chunk]
            else:
                dst[r + i] = value

    def inner(chain):
        for k in range(1, DEPTH + 1):
            for r in range(low + k, high - k, 2):
                relax_rows(chain[k - 1], chain[k], r, 2)

    def outer(chain, dr):
        for k in range(1, DEPTH + 1):
            begin = jnp.where(dr < 0, k, high - k)
            for i in range(0, DEPTH, 2):
                relax_rows(chain[k - 1], chain[k], begin + i, 2)

    def finish_ring(at, count, own_rows):
        for i in range(count):
            r = at + i
            for number, ref in enumerate((first, ground)):
                ring = ring_own[number, i] if own_rows else ring_of(ref, r)
                from_high = jnp.broadcast_to(ring_high[number, r], (SUBL, TILE))
                from_low = jnp.broadcast_to(ring_low[number, r], (SUBL, TILE))
                ring = jnp.where(at_high, from_high, jnp.where(at_low, from_low, ring))
                ref[r, :, chunk:lanes] = ring

    at_high = jnp.logical_and(sub_id == SUBL - 1, right_half)
    at_low = jnp.logical_and(sub_id == 0, jnp.logical_not(right_half))

    adj_load.wait()
    lane_tile = lax.broadcasted_iota(jnp.int32, (n_tiles, padded), 1)
    linked = jnp.zeros((n_tiles, padded), jnp.float32)
    links = adj[...]
    for k in range(links.shape[1]):
        linked = jnp.where(links[:, k : k + 1] == lane_tile, 1.0, linked)
    own = lax.broadcasted_iota(jnp.int32, (n_tiles, padded), 0) == lane_tile
    linked = jnp.where(own, 1.0, linked)
    one_hop = linked
    if n_tiles < padded:
        one_hop = jnp.concatenate(
            [one_hop, jnp.zeros((padded - n_tiles, padded), jnp.float32)], axis=0
        )
    count = jnp.where(own, 0.0, 1.0)
    reach = linked
    for step in range(ROUNDS):
        count = count + (1.0 - reach)
        if step < ROUNDS - 1:
            reach = jnp.dot(reach, one_hop, preferred_element_type=jnp.float32)
            reach = jnp.where(reach > 0.5, 1.0, 0.0)
    hops[...] = count

    for entry in ring_in:
        arrive(entry, True)
    finish_ring(low, height, True)
    chain = (first, ping, pong, ping, second)
    inner(chain)
    row_next = []
    for dr, entries in zip(sides, row_in):
        for entry in entries:
            arrive(entry, False)
        finish_ring(jnp.where(dr < 0, 0, high), DEPTH, False)
        outer(chain, dr)
        row_next.append(rows_out(second, dr, lanes))

    row_in = row_next
    chain = (second, ping, pong, ping, third)
    inner(chain)
    for dr, entry in zip(sides, row_in):
        arrive(entry, False)
        outer(chain, dr)

    first_tile = third[low, :, 0:TILE]
    last_tile = third[low, :, chunk - TILE : chunk]
    for i in range(1, height):
        first_tile = jnp.minimum(first_tile, third[low + i, :, 0:TILE])
        last_tile = jnp.minimum(last_tile, third[low + i, :, chunk - TILE : chunk])
    floor = jnp.minimum(
        jnp.where(first_cell, first_tile, unreached), jnp.where(last_cell, last_tile, unreached)
    )
    for i, counts in ((low, sub == 0), (high - 1, sub == n_sub - 1)):
        skip = jnp.where(counts, -unreached, unreached)
        for j in range(chunk // TILE):
            floor = jnp.minimum(
                floor, jnp.maximum(third[i, :, j * TILE : (j + 1) * TILE], skip)
            )
    floor = jnp.min(floor, axis=(0, 1), keepdims=True)
    tile_id = tile_row * n_cols + col
    mine[...] = jnp.where(
        lax.broadcasted_iota(jnp.int32, (1, padded), 1) == tile_id,
        jnp.broadcast_to(floor, (1, padded)),
        unreached,
    )

    def level_copy(step):
        return pltpu.make_async_remote_copy(
            src_ref=mine,
            dst_ref=gathered.at[members - 1 - step],
            send_sem=level_send,
            recv_sem=level_recv,
            device_id=member((me + step) % members),
            device_id_type=MESH,
        )

    def spread(step, carry):
        level_copy(step).start()
        return carry

    lax.fori_loop(1, members, spread, 0)
    row_in = [rows_out(third, dr, lanes) for dr in (far, near)][::-1]

    chain = (third, ping, pong, ping, done)
    inner(chain)
    for dr, entry in zip(sides, row_in):
        arrive(entry, False)
        outer(chain, dr)

    def seam_of(ref, r):
        ring = ref[r, :, chunk:lanes]
        at_first = jnp.where(right_half, ref[r, :, 0:TILE], ring)
        at_last = jnp.where(right_half, ring, ref[r, :, chunk - TILE : chunk])
        return jnp.where(sub_id == 0, at_first, at_last)

    for r in range(total):
        seam_ground[r] = seam_of(ground, r)

    pltpu.make_async_copy(gathered, gathered, level_recv).wait()
    row = jnp.minimum(mine[...], jnp.min(gathered[...], axis=0))
    count = hops[...]
    best = jnp.full((n_tiles, padded), unreached, jnp.float32)
    for step in range(ROUNDS + 1):
        best = jnp.minimum(
            best, jnp.where(count == float(step), jnp.broadcast_to(row, best.shape), unreached)
        )
        row = row + hop_rise
    level = jnp.min(best, axis=1, keepdims=True)
    levels[...] = jnp.broadcast_to(level + spill_lift, levels.shape)

    def ceiling(row_at, col_at):
        at = jnp.clip(row_at, 0, n_rows - 1) * n_cols + jnp.clip(col_at, 0, n_cols - 1)
        return jnp.broadcast_to(levels[pl.ds(at, 1)], (SUBL, TILE))

    def ceilings(row_at):
        here = ceiling(row_at, col)
        beside = jnp.where(
            at_high, ceiling(row_at, col + 1), jnp.where(at_low, ceiling(row_at, col - 1), here)
        )
        return here, beside

    above, own_row, below = (ceilings((band + dr + n_sub) // n_sub - 1) for dr in (-1, 0, 1))
    beyond = ceilings((band + far + n_sub) // n_sub - 1)

    seam = []
    for r in range(total):
        top = (above if r < low else own_row if r < high else below)[1]
        seam.append(jnp.maximum(seam_ground[r], top))
    for k in range(1, DEPTH + 1):
        later = list(seam)
        for r in range(k, total - k):
            low3 = jnp.minimum(jnp.minimum(seam[r - 1], seam[r + 1]), seam[r])
            least = jnp.minimum(
                low3, jnp.minimum(pltpu.roll(low3, 1, 1), pltpu.roll(low3, TILE - 1, 1))
            )
            later[r] = jnp.maximum(seam_ground[r], jnp.minimum(seam[r], least + rise_step))
        seam = later
    for i in range(height):
        seam_ground[low + i] = seam[low + i]

    def flat(at, count, tops, targets):
        here, beside = tops
        for i in range(count):
            for j in range(lanes // TILE):
                cut = slice(j * TILE, (j + 1) * TILE)
                top = beside if j == lanes // TILE - 1 else here
                value = jnp.maximum(ground[at + i, :, cut], top)
                for target in targets:
                    target[at + i, :, cut] = value

    flat(jnp.where(far < 0, 0, high), DEPTH, beyond, (even,))
    flat(jnp.where(far < 0, low, high - DEPTH - 1), DEPTH + 1, own_row, (even, odd))
    outer((even, odd, even, odd, even), far)

    left_seam = jnp.logical_and(sub_id == 0, lane_id < DEPTH)
    right_seam = jnp.logical_and(sub_id == SUBL - 1, lane_id >= TILE - DEPTH)

    def merge(at, count, is_far):
        for i in range(count):
            r = at + i
            for j in range(chunk // TILE):
                cut = slice(j * TILE, (j + 1) * TILE)
                top = even[r, :, cut] if is_far else jnp.maximum(ground[r, :, cut], own_row[0])
                value = jnp.minimum(done[r - low, :, cut], top)
                if j == 0:
                    value = jnp.where(left_seam, jnp.minimum(value, seam_ground[r]), value)
                if j == chunk // TILE - 1:
                    value = jnp.where(right_seam, jnp.minimum(value, seam_ground[r]), value)
                done[r - low, :, cut] = value

    merge(jnp.where(far < 0, low + DEPTH, low), height - DEPTH, False)
    merge(jnp.where(far < 0, low, high - DEPTH), DEPTH, True)

    for s in range(SUBL):
        pltpu.make_async_copy(
            done.at[:, s], out_hbm.at[:, pl.ds(s * chunk, chunk)], out_sem
        ).start()
    for copy, dr, dc in copies:
        pl.when(both(dr, dc))(copy.wait_send)
    pltpu.make_async_copy(gathered, gathered, level_send).wait()
    pltpu.make_async_copy(done, done, out_sem).wait()


def per_device(sizes, elevation, fill_depth, edge_rows, edge_sides, adjacency):
    height, width = elevation.shape
    chunk = width // SUBL
    total = height + 2 * DEPTH
    members = sizes[1] * sizes[2] * sizes[3]
    n_tiles = adjacency.shape[0]
    padded = -(-n_tiles // TILE) * TILE
    wide = pltpu.VMEM((total, SUBL, chunk + TILE), jnp.float32)
    own = pltpu.VMEM((height, SUBL, chunk), jnp.float32)
    ring = pltpu.VMEM((2, total, 1, TILE), jnp.float32)
    return pl.pallas_call(
        functools.partial(kernel, sizes),
        out_shape=jax.ShapeDtypeStruct((height, width), jnp.float32),
        in_specs=[pl.BlockSpec(memory_space=pltpu.HBM)] * 5,
        out_specs=pl.BlockSpec(memory_space=pl.ANY),
        scratch_shapes=[
            wide, own, wide, wide, wide, wide, wide, own,
            pltpu.VMEM((2, SUBL, chunk), jnp.int32),
            pltpu.SMEM(edge_sides.shape, jnp.int32),
            pltpu.VMEM(adjacency.shape, jnp.int32),
            pltpu.VMEM((2, height, SUBL, TILE), jnp.float32),
            ring, ring,
            pltpu.VMEM((1, padded), jnp.float32),
            pltpu.VMEM((members - 1, 1, padded), jnp.float32),
            pltpu.VMEM((n_tiles, padded), jnp.float32),
            pltpu.VMEM((n_tiles, TILE), jnp.float32),
            wide, wide,
            pltpu.VMEM((total, SUBL, TILE), jnp.float32),
            pltpu.SemaphoreType.DMA((5,)),
            pltpu.SemaphoreType.DMA((14,)),
            pltpu.SemaphoreType.DMA((14,)),
            pltpu.SemaphoreType.DMA,
            pltpu.SemaphoreType.DMA,
            pltpu.SemaphoreType.DMA,
        ],
        compiler_params=pltpu.CompilerParams(
            collective_id=0, has_side_effects=True, vmem_limit_bytes=32 * 1024 * 1024
        ),
    )(elevation, fill_depth, edge_rows, edge_sides, adjacency)


def solution(mesh):
    sizes = tuple(mesh.shape[name] for name in ("groups", "rows", "cols", "sub"))
    placed = (
        P(("groups", "rows", "sub"), "cols"),
        P(("groups", "rows", "sub"), "cols"),
        P("groups", "cols"),
        P("groups", ("rows", "sub")),
        P("groups", None),
    )
    return jax.shard_map(
        functools.partial(per_device, sizes),
        mesh=mesh,
        in_specs=placed,
        out_specs=P(("groups", "rows", "sub"), "cols"),
        check_vma=False,
    )
```
